32 devices in a mesh: grp: 2 (over y), ha: 4 (over z), wa: 2 (over x), ta: 2 (over core).
Axes of the slice: x: 2, y: 2, z: 4, core: 2. Of those that a mesh axis runs over, the one named last changes fastest.
Arguments:
- frames: bfloat16 [8, 96, 16, 256], P(('grp', 'ta'), None, 'ha', 'wa'), parts along dimension 0, may hold values from -14 to 14
- cache_in: bfloat16 [4, 96, 16, 256], P('grp', None, 'ha', 'wa'), parts along dimension 0, may hold values from -4 to 4
- cache_mid: bfloat16 [4, 96, 16, 256], P('grp', None, 'ha', 'wa'), parts along dimension 0, may hold values from -4 to 4
- gain_in: float32 [96], replicated, may hold values from 0.25 to 1.75
- gain_mid: float32 [96], replicated, may hold values from 0.25 to 1.75
- weight_in: bfloat16 [3, 3, 96, 288], replicated, may hold values from -0.125 to 0.125
- bias_in: float32 [96], replicated, may hold values from -3 to 3
- weight_mid: bfloat16 [3, 3, 96, 288], replicated, may hold values from -0.125 to 0.125
- bias_mid: float32 [96], replicated, may hold values from -3 to 3
- cotangent: bfloat16 [8, 96, 16, 256], P(('grp', 'ta'), None, 'ha', 'wa'), parts along dimension 0, may hold values from -6 to 6
Outputs:
- decoded: bfloat16 [8, 96, 16, 256], P(('grp', 'ta'), None, 'ha', 'wa'), parts along dimension 0
- input_grad: float32 [8, 96, 16, 256], P(('grp', 'ta'), None, 'ha', 'wa'), parts along dimension 0
The draws below stay inside these ranges and needn't reach their ends.
There are 2 independent parts, one for each index of `grp`. The reference program is written for one: setup_inputs(seed, part) draws one part's arguments, and reference() takes and returns one part's arrays. A program takes and returns all parts, laid end to end along the dimension named above; an argument that names none is the same for every part. Nothing has to cross between parts.
All inputs are finite; a program needn't handle non-finite values.
Results may differ from the reference program's by a relative error of at most 0.006.
Values may be sent and summed in bfloat16 or wider, within the bound.
A program may use at most 64 MiB of HBM per device.

```python
import jax
import jax.numpy as jnp
from jax import lax

C = 96
F = 4
H = 16
W = 256


def draw_frames(key, part):
    key_base = jax.random.fold_in(key, 11)
    key_scale = jax.random.fold_in(key, 12)
    base = jax.random.truncated_normal(key_base, -4.0, 4.0, (F, C, H, W), jnp.float32)
    scales = jnp.exp(jax.random.uniform(key_scale, (F, 1, H, W), jnp.float32, -1.2, 1.2))
    return (base * scales).astype(jnp.bfloat16)


def steps_of(stream_key, extent, cuts, least, top_value):
    level = 1.0
    for dim, blocks in cuts:
        draws = jax.random.uniform(jax.random.fold_in(jax.random.fold_in(stream_key, 6), dim), (blocks,), jnp.float32, least / len(cuts), top_value / len(cuts))
        level = level * jnp.repeat(jnp.exp(draws), extent[dim] // blocks).reshape((-1,) + (1,) * (len(extent) - 1 - dim))
    return level


def noise(own_key, extent, scale, bound, pieces=(), held_as=jnp.bfloat16):
    array = scale * jax.random.normal(own_key, extent, jnp.float32)
    if pieces:
        array = array * steps_of(own_key, extent, pieces, -0.22, 0.18)
    return jnp.clip(array, -bound, bound).astype(held_as)


def setup_inputs(seed: int = 0, part: int = 0) -> dict:
    seeds = jax.random.split(jax.random.key(seed), 11)
    own_keys = jax.random.split(jax.random.fold_in(seeds[10], part), 11)
    return {
        "frames": draw_frames(jax.random.fold_in(jax.random.fold_in(seeds[10], part), 71), part),
        "cache_in": noise(own_keys[1], (2, C, H, W), 0.7, 4.0, ((2, 4), (3, 2))),
        "cache_mid": noise(own_keys[2], (2, C, H, W), 0.7, 4.0, ((2, 4), (3, 2))),
        "gain_in": jnp.clip(1.0 + 0.15 * jax.random.normal(seeds[3], (C,), jnp.float32), 0.25, 1.75),
        "gain_mid": jnp.clip(1.0 + 0.15 * jax.random.normal(seeds[4], (C,), jnp.float32), 0.25, 1.75),
        "weight_in": noise(seeds[5], (3, 3, C, 3 * C), (27 * C) ** -0.5, 0.125),
        "bias_in": noise(seeds[6], (C,), 0.5, 3.0, (), jnp.float32),
        "weight_mid": noise(seeds[7], (3, 3, C, 3 * C), (27 * C) ** -0.5, 0.125),
        "bias_mid": noise(seeds[8], (C,), 0.5, 3.0, (), jnp.float32),
        "cotangent": noise(own_keys[9], (F, C, H, W), 1.0, 6.0, ((0, 2), (2, 4), (3, 2))),
    }


epsilon = 1e-06

def activate(values, gain):
    values = values.astype(jnp.float32)
    mean_square = lax.optimization_barrier(jnp.mean(values * values, axis=1, keepdims=True))
    scaled = values * lax.rsqrt(mean_square + epsilon) * gain[None, :, None, None]
    return jax.nn.silu(scaled)

def act_back(values, gain, upstream):
    values = values.astype(jnp.float32)
    mean_square = lax.optimization_barrier(jnp.mean(values * values, axis=1, keepdims=True))
    inverse = lax.rsqrt(mean_square + epsilon)
    gains = gain[None, :, None, None]
    scaled = values * inverse * gains
    sigmoid_part = jax.nn.sigmoid(scaled)
    weighted = gains * upstream * sigmoid_part * (1.0 + scaled * (1.0 - sigmoid_part))
    return inverse * weighted - values * inverse ** 3 * lax.optimization_barrier(jnp.mean(weighted * values, axis=1, keepdims=True))

def flipped(weight):
    channels = weight.shape[2]
    five = weight.reshape(3, 3, channels, 3, channels)[::-1, ::-1, :, ::-1, :]
    return jnp.transpose(five, (0, 1, 4, 3, 2)).reshape(3, 3, channels, 3 * channels)

def pad_grid(values):
    return jnp.pad(values, ((0, 0), (0, 0), (1, 1), (1, 1)))

def convolve(padded, weight):
    count_frames = padded.shape[0] - 2
    height = padded.shape[2] - 2
    width = padded.shape[3] - 2
    weights = weight.astype(jnp.float32)

    def one_frame(index_frame):
        parts = [lax.dynamic_slice_in_dim(padded, index_frame + time_tap, 1, 0)[0] for time_tap in range(3)]
        stacked = jnp.concatenate(parts, 0).astype(jnp.float32)
        summed = jnp.zeros((weight.shape[2], height, width), jnp.float32)
        for row_tap in range(3):
            for col_tap in range(3):
                summed = summed + jnp.einsum('ok,khw->ohw', weights[row_tap, col_tap], stacked[:, row_tap:row_tap + height, col_tap:col_tap + width])
        return summed
    return lax.map(one_frame, jnp.arange(count_frames, dtype=jnp.int32))

def reference(frames, cache_in, cache_mid, gain_in, gain_mid, weight_in, bias_in, weight_mid, bias_mid, cotangent):
    active_in = activate(frames, gain_in).astype(jnp.bfloat16)
    padded_in = pad_grid(jnp.concatenate([cache_in, active_in], 0))
    hidden = (convolve(padded_in, weight_in) + bias_in[None, :, None, None]).astype(jnp.bfloat16)
    active_mid = activate(hidden, gain_mid).astype(jnp.bfloat16)
    padded_mid = pad_grid(jnp.concatenate([cache_mid, active_mid], 0))
    residual = convolve(padded_mid, weight_mid) + bias_mid[None, :, None, None]
    decoded = (frames.astype(jnp.float32) + residual).astype(jnp.bfloat16)
    no_frames = jnp.zeros((2,) + cotangent.shape[1:], jnp.bfloat16)
    back_mid = convolve(pad_grid(jnp.concatenate([cotangent, no_frames], 0)), flipped(weight_mid))
    d_hidden = act_back(hidden, gain_mid, back_mid).astype(jnp.bfloat16)
    back_in = convolve(pad_grid(jnp.concatenate([d_hidden, no_frames], 0)), flipped(weight_in))
    input_grad = cotangent.astype(jnp.float32) + act_back(frames, gain_in, back_in)
    return (decoded, input_grad)
```

```python
import functools

import jax
import jax.numpy as jnp
from jax import lax
from jax.experimental import pallas as pl
from jax.experimental.pallas import tpu as pltpu
from jax.sharding import PartitionSpec as P

epsilon = 1e-06
BF, F32 = jnp.bfloat16, jnp.float32


def act(v, g):
    m = jnp.mean(v * v, axis=0, keepdims=True)
    z = v * lax.rsqrt(m + epsilon) * g
    return z * (1.0 / (1.0 + jnp.exp(-z)))


def act_back(v, g, d):
    m = jnp.mean(v * v, axis=0, keepdims=True)
    r = lax.rsqrt(m + epsilon)
    z = v * r * g
    s = 1.0 / (1.0 + jnp.exp(-z))
    q = g * d * s * (1.0 + z * (1.0 - s))
    return r * q - v * (r * r * r) * jnp.mean(q * v, axis=0, keepdims=True)


def kernel(
    n_ha, n_wa, x, w_in, w_mid, par, dec, grad,
    cb_in, cb_cot, cb_mid, cb_back, eb, e_out, stack, wts, acc, hid, send, recv,
):
    _, nf, nh, ch, nw = x.shape
    np_ = nh + 2
    ha, wa, ta = (lax.axis_index(a) for a in ("ha", "wa", "ta"))
    first, second = ta == 0, ta == 1
    lane = lax.broadcasted_iota(jnp.int32, (ch, nw), 1)
    half = nw // 2
    slot_row = lane % 8

    def have(dh, dw):
        ok = None
        for step, me, count in ((dh, ha, n_ha), (dw, wa, n_wa)):
            if step:
                this = (me > 0) if step < 0 else (me < count - 1)
                ok = this if ok is None else jnp.logical_and(ok, this)
        return ok

    def both(a, b):
        return b if a is None else a if b is None else jnp.logical_and(a, b)

    def when(cond, fn):
        if cond is None:
            fn()
        else:
            pl.when(cond)(fn)

    def target(dh, dw, dt):
        ids = {}
        if dh:
            ids["ha"] = ha + dh
        if dw:
            ids["wa"] = wa + dw
        if dt:
            ids["ta"] = 1 - ta
        return ids

    steps = [(dh, dw) for dh in (-1, 0, 1) for dw in (-1, 0, 1)]
    barrier = pltpu.get_barrier_semaphore()
    for dh, dw in steps:
        for dt in (0, 1):
            if dh or dw or dt:
                when(
                    have(dh, dw),
                    lambda dh=dh, dw=dw, dt=dt: pl.semaphore_signal(
                        barrier, inc=1, device_id=target(dh, dw, dt),
                        device_id_type=pl.DeviceIdType.MESH,
                    ),
                )
    rows_near = 1 + (ha > 0).astype(jnp.int32) + (ha < n_ha - 1).astype(jnp.int32)
    cols_near = 1 + (wa > 0).astype(jnp.int32) + (wa < n_wa - 1).astype(jnp.int32)

    used = [0]

    def transfer(src, dst, dh, dw, dt, sender=None, receiver=None):
        k = used[0]
        used[0] += 1
        copy = pltpu.make_async_remote_copy(
            src_ref=src, dst_ref=dst, send_sem=send.at[k], recv_sem=recv.at[k],
            device_id=target(dh, dw, dt), device_id_type=pl.DeviceIdType.MESH,
        )
        return copy, both(have(dh, dw), sender), both(have(-dh, -dw), receiver)

    def start(items):
        for copy, s, _ in items:
            when(s, copy.start)

    def arrive(items):
        for copy, _, r in items:
            when(r, copy.wait_recv)

    def leave(items):
        for copy, s, _ in items:
            when(s, copy.wait_send)

    def rows_of(top, bottom, cb, g, dt, sender=None, receiver=None):
        return [
            transfer(bottom, cb.at[g, :, 0], 1, 0, dt, sender, receiver),
            transfer(top, cb.at[g, :, nh + 1], -1, 0, dt, sender, receiver),
        ]

    def edges_of(stage, g, dt, sender=None, receiver=None):
        return [
            transfer(
                e_out.at[stage], eb.at[stage, g, 1 - dh, (dw + 1) // 2], dh, dw, dt,
                sender, receiver,
            )
            for dh, dw in steps if dw
        ]

    def make_edges(stage, tiles):
        e = jnp.zeros((ch, nw), F32)
        for (arr, f, h), tile in tiles:
            j = arr * 16 + f * 8 + h + 1
            e = jnp.where(lane == j, tile[:, :1], e)
            e = jnp.where(lane == half + j, tile[:, nw - 1 :], e)
        e_out[stage] = e.astype(BF)

    up, down, left, right = have(-1, 0), have(1, 0), have(0, -1), have(0, 1)

    def flag(cond):
        return jnp.full((ch, nw), cond.astype(jnp.int32), jnp.int32)

    side_ok = jnp.where(lane < half, flag(right), flag(left))
    row_ok = jnp.where(slot_row == 0, flag(up), jnp.where(slot_row == nh + 1, flag(down), 1))
    edge_ok = (side_ok * row_ok) > 0

    def merged(stage, g):
        v = [
            jnp.where(lane < half, eb[stage, g, s, 0].astype(F32), eb[stage, g, s, 1].astype(F32))
            for s in range(3)
        ]
        return jnp.where(
            slot_row == 0,
            pltpu.roll(v[0], nw - nh, 1),
            jnp.where(slot_row == nh + 1, pltpu.roll(v[2], nh, 1), v[1]),
        )

    first_tile, up_tile, down_tile = flag(first) > 0, flag(up) > 0, flag(down) > 0

    def put(conv, fp, hp, tile, edge, j):
        base = hp * 3 * ch
        if hp == 0:
            tile = jnp.where(up_tile, tile, 0.0)
        if hp == nh + 1:
            tile = jnp.where(down_tile, tile, 0.0)
        le = jnp.where(lane == 0, edge[:, half + j : half + j + 1], pltpu.roll(tile, 1, 1))
        ri = jnp.where(lane == nw - 1, edge[:, j : j + 1], pltpu.roll(tile, nw - 1, 1))
        stack[conv, fp, base : base + ch] = le.astype(BF)
        stack[conv, fp, base + ch : base + 2 * ch] = tile.astype(BF)
        stack[conv, fp, base + 2 * ch : base + 3 * ch] = ri.astype(BF)

    def convolve(conv, weight):
        for fp in range(nf + 2):
            taps = [t for t in range(3) if 0 <= fp - t < nf]
            lo, hi = taps[0] * ch, (taps[-1] + 1) * ch
            lhs = wts[weight, lo:hi]
            for h in range(0, nh, 2):
                a = stack[conv, fp, h * 3 * ch : (h + 3) * 3 * ch]
                b = stack[conv, fp, (h + 1) * 3 * ch : (h + 4) * 3 * ch]
                out = jnp.dot(
                    lhs, jnp.concatenate([a, b], axis=1), preferred_element_type=F32
                )
                for i, t in enumerate(taps):
                    f = fp - t
                    for k in range(2):
                        part = out[i * ch : (i + 1) * ch, k * nw : (k + 1) * nw]
                        if t == 0:
                            acc[f, h + k] = part
                        else:
                            acc[f, h + k] += part

    g_in, g_mid, b_in, b_mid = (par[:, i : i + 1] for i in range(4))

    own = [(f, h) for f in range(nf) for h in range(nh)]
    make_edges(0, [((a, f, h), x[a, f, h].astype(F32)) for a in range(4) for f, h in own])
    pl.semaphore_wait(barrier, 2 * rows_near * cols_near - 1)

    def x_rows(a, cb, g, dt, sender=None, receiver=None):
        return rows_of(x.at[a, :, 0], x.at[a, :, nh - 1], cb, g, dt, sender, receiver)

    e_own = edges_of(0, 0, 0)
    e_other = edges_of(0, 1, 1)
    s_cot = x_rows(3, cb_cot, 0, 0)
    s_cot += x_rows(3, cb_cot, 1, 1, second, first)
    s_cot += [transfer(x.at[3], cb_cot.at[1, :, 1 : nh + 1], 0, 0, 1, second, first)]
    s_in = x_rows(0, cb_in, 0, 0)
    s_in += x_rows(0, cb_in, 1, 1, first, second)
    s_in += [transfer(x.at[0], cb_in.at[1, :, 1 : nh + 1], 0, 0, 1, first, second)]
    s_in += x_rows(1, cb_in, 1, 0, first, first)
    s_cache = x_rows(2, cb_mid, 1, 0, first, first)
    stage0 = e_own + e_other + s_cot + s_in + s_cache
    start(stage0)

    for fwd, w in ((0, w_in), (1, w_mid)):
        for ab in range(9):
            block = w[ab].astype(F32)
            turned = w[8 - ab].astype(F32).T
            for t in range(3):
                wts[fwd, t * ch : (t + 1) * ch, ab * ch : (ab + 1) * ch] = block[
                    :, t * ch : (t + 1) * ch
                ].astype(BF)
                wts[2 + fwd, t * ch : (t + 1) * ch, ab * ch : (ab + 1) * ch] = turned[
                    (2 - t) * ch : (3 - t) * ch
                ].astype(BF)

    arrive(e_own + e_other + s_cot)
    raw_own, raw_other = merged(0, 0), merged(0, 1)
    e0 = jnp.where(edge_ok, raw_own, 0.0)
    e1 = jnp.where(edge_ok, jnp.where(first_tile, raw_other, 0.0), 0.0)
    for f in range(nf):
        for hp in range(np_):
            j = 3 * 16 + f * 8 + hp
            inner = 1 <= hp <= nh
            tile = x[3, f, hp - 1] if inner else cb_cot[0, f, hp]
            put(0, f, hp, tile.astype(F32), e0, j)
            tile = jnp.where(first_tile, cb_cot[1, f, hp].astype(F32), 0.0)
            put(0, nf + f, hp, tile, e1, j)
    convolve(0, 3)
    for f, h in own:
        grad[f, h] = acc[f, h]

    arrive(s_in)
    e_in0 = jnp.where(edge_ok, act(raw_own, g_in), 0.0)
    e_in1 = jnp.where(
        edge_ok,
        jnp.where(first_tile, pltpu.roll(raw_own, nw - 16, 1), act(raw_other, g_in)),
        0.0,
    )
    for f in range(nf):
        for hp in range(np_):
            j = f * 8 + hp
            inner = 1 <= hp <= nh
            tile = x[0, f, hp - 1] if inner else cb_in[0, f, hp]
            put(1, nf + f, hp, act(tile.astype(F32), g_in), e_in0, j)
            there = cb_in[1, f, hp].astype(F32)
            here = x[1, f, hp - 1].astype(F32) if inner else there
            put(1, f, hp, jnp.where(first_tile, here, act(there, g_in)), e_in1, j)
    convolve(1, 0)
    tiles = []
    for f, h in own:
        hidden = (acc[f, h] + b_in).astype(BF)
        hid[f, h] = hidden
        a = act(hidden.astype(F32), g_mid).astype(BF)
        cb_mid[0, f, h + 1] = a
        tiles.append(((0, f, h), a.astype(F32)))
    make_edges(1, tiles)

    def later(stage, cb, sender, receiver):
        top, bottom = cb.at[0, :, 1], cb.at[0, :, nh]
        items = edges_of(stage, 0, 0) + rows_of(top, bottom, cb, 0, 0)
        items += edges_of(stage, 1, 1, sender, receiver)
        items += rows_of(top, bottom, cb, 1, 1, sender, receiver)
        items += [
            transfer(
                cb.at[0, :, 1 : nh + 1], cb.at[1, :, 1 : nh + 1], 0, 0, 1, sender, receiver
            )
        ]
        return items

    stage1 = later(1, cb_mid, first, second)
    start(stage1)

    tiles = []
    for f, h in own:
        d = act_back(hid[f, h].astype(F32), g_mid, grad[f, h]).astype(BF)
        cb_back[0, f, h + 1] = d
        tiles.append(((0, f, h), d.astype(F32)))
    make_edges(2, tiles)
    stage2 = later(2, cb_back, second, first)
    start(stage2)

    arrive(s_cache)
    arrive(stage1)
    e0 = jnp.where(edge_ok, merged(1, 0), 0.0)
    e1 = jnp.where(
        edge_ok, jnp.where(first_tile, pltpu.roll(raw_own, nw - 32, 1), merged(1, 1)), 0.0
    )
    for f in range(nf):
        for hp in range(np_):
            j = f * 8 + hp
            inner = 1 <= hp <= nh
            put(2, nf + f, hp, cb_mid[0, f, hp].astype(F32), e0, j)
            there = cb_mid[1, f, hp].astype(F32)
            if inner:
                there = jnp.where(first_tile, x[2, f, hp - 1].astype(F32), there)
            put(2, f, hp, there, e1, j)
    convolve(2, 1)
    for f, h in own:
        dec[f, h] = (x[0, f, h].astype(F32) + acc[f, h] + b_mid).astype(BF)

    arrive(stage2)
    e0 = jnp.where(edge_ok, merged(2, 0), 0.0)
    e1 = jnp.where(edge_ok, jnp.where(first_tile, merged(2, 1), 0.0), 0.0)
    for f in range(nf):
        for hp in range(np_):
            j = f * 8 + hp
            put(3, f, hp, cb_back[0, f, hp].astype(F32), e0, j)
            tile = jnp.where(first_tile, cb_back[1, f, hp].astype(F32), 0.0)
            put(3, nf + f, hp, tile, e1, j)
    convolve(3, 2)
    for f, h in own:
        grad[f, h] = x[3, f, h].astype(F32) + act_back(x[0, f, h].astype(F32), g_in, acc[f, h])
    leave(stage0 + stage1 + stage2)


def per_device(
    frames, cache_in, cache_mid, gain_in, gain_mid, weight_in, bias_in, weight_mid,
    bias_mid, cotangent,
):
    nf, ch, nh, nw = frames.shape
    x = jnp.stack([frames, cache_in, cache_mid, cotangent]).transpose(0, 1, 3, 2, 4)
    par = jnp.stack([gain_in, gain_mid, bias_in, bias_mid], 1)
    k = 3 * ch
    vmem = pl.BlockSpec(memory_space=pltpu.VMEM)
    center = pltpu.VMEM((2, nf, nh + 2, ch, nw), BF)
    copies = 96
    dec, grad = pl.pallas_call(
        functools.partial(kernel, lax.axis_size("ha"), lax.axis_size("wa")),
        out_shape=(
            jax.ShapeDtypeStruct((nf, nh, ch, nw), BF),
            jax.ShapeDtypeStruct((nf, nh, ch, nw), F32),
        ),
        in_specs=[vmem] * 4,
        out_specs=(vmem, vmem),
        scratch_shapes=[
            center, center, center, center,
            pltpu.VMEM((3, 2, 3, 2, ch, nw), BF),
            pltpu.VMEM((3, ch, nw), BF),
            pltpu.VMEM((4, nf + 2, (nh + 2) * k, nw), BF),
            pltpu.VMEM((4, k, 9 * ch), BF),
            pltpu.VMEM((nf, nh, ch, nw), F32),
            pltpu.VMEM((nf, nh, ch, nw), BF),
            pltpu.SemaphoreType.DMA((copies,)),
            pltpu.SemaphoreType.DMA((copies,)),
        ],
        compiler_params=pltpu.CompilerParams(
            collective_id=0, has_side_effects=True, vmem_limit_bytes=60 << 20
        ),
    )(x, weight_in.reshape(9, ch, k), weight_mid.reshape(9, ch, k), par)
    return dec.transpose(0, 2, 1, 3), grad.transpose(0, 2, 1, 3)


def solution(mesh):
    moving = P(("grp", "ta"), None, "ha", "wa")
    cache = P("grp", None, "ha", "wa")
    placed = (moving, cache, cache, P(), P(), P(), P(), P(), P(), moving)
    return jax.shard_map(
        per_device, mesh=mesh, in_specs=placed, out_specs=(moving, moving), check_vma=False
    )
```

```python
import functools

import jax
import jax.numpy as jnp
from jax import lax
from jax.experimental import pallas as pl
from jax.experimental.pallas import tpu as pltpu
from jax.sharding import PartitionSpec as P

epsilon = 1e-06
BF, F32 = jnp.bfloat16, jnp.float32


def act(v, g):
    m = jnp.mean(v * v, axis=0, keepdims=True)
    z = v * lax.rsqrt(m + epsilon) * g
    return z * (1.0 / (1.0 + jnp.exp(-z)))


def act_back(v, g, d):
    m = jnp.mean(v * v, axis=0, keepdims=True)
    r = lax.rsqrt(m + epsilon)
    z = v * r * g
    s = 1.0 / (1.0 + jnp.exp(-z))
    q = g * d * s * (1.0 + z * (1.0 - s))
    return r * q - v * (r * r * r) * jnp.mean(q * v, axis=0, keepdims=True)


def kernel(
    n_ha, n_wa, x0, x1, x2, x3, w_in, w_mid, p0, p1, p2, p3, dec, grad,
    cb_in, cb_cot, cb_mid, cb_back, eb0, eb, e_out0, e_out, stack, wts, acc, wide,
    hid, send, recv,
):
    x = (x0, x1, x2, x3)
    nf, nh, ch, nw = x0.shape
    fold = 16
    np_ = nh + 2
    ha, wa, ta = (lax.axis_index(a) for a in ("ha", "wa", "ta"))
    first, second = ta == 0, ta == 1
    lane = lax.broadcasted_iota(jnp.int32, (ch, nw), 1)
    half = nw // 2
    small_lane = lax.broadcasted_iota(jnp.int32, (fold, nw), 1)
    small_row = small_lane % 8
    slot_row = lane % 8

    def have(dh, dw):
        ok = None
        for step, me, count in ((dh, ha, n_ha), (dw, wa, n_wa)):
            if step:
                this = (me > 0) if step < 0 else (me < count - 1)
                ok = this if ok is None else jnp.logical_and(ok, this)
        return ok

    def both(a, b):
        return b if a is None else a if b is None else jnp.logical_and(a, b)

    def when(cond, fn):
        if cond is None:
            fn()
        else:
            pl.when(cond)(fn)

    def target(dh, dw, dt):
        ids = {}
        if dh:
            ids["ha"] = ha + dh
        if dw:
            ids["wa"] = wa + dw
        if dt:
            ids["ta"] = 1 - ta
        return ids

    steps = [(dh, dw) for dh in (-1, 0, 1) for dw in (-1, 0, 1)]
    barrier = pltpu.get_barrier_semaphore()
    for dh, dw in steps:
        for dt in (0, 1):
            if dh or dw or dt:
                when(
                    have(dh, dw),
                    lambda dh=dh, dw=dw, dt=dt: pl.semaphore_signal(
                        barrier, inc=1, device_id=target(dh, dw, dt),
                        device_id_type=pl.DeviceIdType.MESH,
                    ),
                )
    rows_near = 1 + (ha > 0).astype(jnp.int32) + (ha < n_ha - 1).astype(jnp.int32)
    cols_near = 1 + (wa > 0).astype(jnp.int32) + (wa < n_wa - 1).astype(jnp.int32)

    used = [0]

    def transfer(src, dst, dh, dw, dt, sender=None, receiver=None):
        k = used[0]
        used[0] += 1
        copy = pltpu.make_async_remote_copy(
            src_ref=src, dst_ref=dst, send_sem=send.at[k], recv_sem=recv.at[k],
            device_id=target(dh, dw, dt), device_id_type=pl.DeviceIdType.MESH,
        )
        return copy, both(have(dh, dw), sender), both(have(-dh, -dw), receiver)

    def start(items):
        for copy, s, _ in items:
            when(s, copy.start)

    def arrive(items):
        for copy, _, r in items:
            when(r, copy.wait_recv)

    def leave(items):
        for copy, s, _ in items:
            when(s, copy.wait_send)

    def rows_of(top, bottom, cb, g, dt, sender=None, receiver=None):
        return [
            transfer(bottom, cb.at[g, :, 0], 1, 0, dt, sender, receiver),
            transfer(top, cb.at[g, :, nh + 1], -1, 0, dt, sender, receiver),
        ]

    def edges_of(source, landing, dt, sender=None, receiver=None):
        return [
            transfer(
                source((dw + 1) // 2), landing(1 - dh, (dw + 1) // 2), dh, dw, dt,
                sender, receiver,
            )
            for dh, dw in steps if dw
        ]

    def make_edges(tiles):
        e = jnp.zeros((ch, nw), F32)
        for (f, h), tile in tiles:
            j = f * 8 + h + 1
            e = jnp.where(lane == j, tile[:, :1], e)
            e = jnp.where(lane == half + j, tile[:, nw - 1 :], e)
        out = []
        for side in range(2):
            c = jnp.zeros((fold, nw), F32)
            for i in range(ch // fold):
                part = e[i * fold : (i + 1) * fold]
                shift = (i * 16 - half * side) % nw
                part = pltpu.roll(part, shift, 1) if shift else part
                c = jnp.where(small_lane // 16 == i, part, c)
            out.append(c.astype(BF))
        return out

    up, down, left, right = have(-1, 0), have(1, 0), have(0, -1), have(0, 1)

    def flag(cond):
        return jnp.full((ch, nw), cond.astype(jnp.int32), jnp.int32)

    side_ok = jnp.where(lane < half, flag(right), flag(left))
    row_ok = jnp.where(slot_row == 0, flag(up), jnp.where(slot_row == nh + 1, flag(down), 1))
    edge_ok = (side_ok * row_ok) > 0

    def merged(landing):
        sides = []
        for side in range(2):
            v = [landing(s, side)[...].astype(F32) for s in range(3)]
            m = jnp.where(
                small_row == 0,
                pltpu.roll(v[0], nw - nh, 1),
                jnp.where(small_row == nh + 1, pltpu.roll(v[2], nh, 1), v[1]),
            )
            shifts = [(half * side - i * 16) % nw for i in range(ch // fold)]
            sides.append(
                jnp.concatenate([pltpu.roll(m, t, 1) if t else m for t in shifts], axis=0)
            )
        return jnp.where(lane < half, sides[0], sides[1])

    first_tile, up_tile, down_tile = flag(first) > 0, flag(up) > 0, flag(down) > 0

    def put(conv, fp, hp, tile, edge, j):
        base = hp * 3 * ch
        if hp == 0:
            tile = jnp.where(up_tile, tile, 0.0)
        if hp == nh + 1:
            tile = jnp.where(down_tile, tile, 0.0)
        le = jnp.where(lane == 0, edge[:, half + j : half + j + 1], pltpu.roll(tile, 1, 1))
        ri = jnp.where(lane == nw - 1, edge[:, j : j + 1], pltpu.roll(tile, nw - 1, 1))
        stack[conv, fp, base : base + ch] = le.astype(BF)
        stack[conv, fp, base + ch : base + 2 * ch] = tile.astype(BF)
        stack[conv, fp, base + 2 * ch : base + 3 * ch] = ri.astype(BF)

    def convolve(conv, weight):
        for fp in range(nf + 2):
            taps = [t for t in range(3) if 0 <= fp - t < nf]
            lo, hi = taps[0] * ch, (taps[-1] + 1) * ch
            lhs = wts[weight, lo:hi]
            for h in range(0, nh, 2):
                a = stack[conv, fp, h * 3 * ch : (h + 3) * 3 * ch]
                b = stack[conv, fp, (h + 1) * 3 * ch : (h + 4) * 3 * ch]
                out = jnp.dot(
                    lhs, jnp.concatenate([a, b], axis=1), preferred_element_type=F32
                )
                for i, t in enumerate(taps):
                    f = fp - t
                    for k in range(2):
                        part = out[i * ch : (i + 1) * ch, k * nw : (k + 1) * nw]
                        if t == 0:
                            acc[f, h + k] = part
                        else:
                            acc[f, h + k] += part

    eye = lax.broadcasted_iota(jnp.int32, (ch, ch), 0) == lax.broadcasted_iota(
        jnp.int32, (ch, ch), 1
    )
    g_in, g_mid, b_in, b_mid = (
        jnp.sum(jnp.where(eye, p[...], 0.0), axis=1, keepdims=True) for p in (p0, p1, p2, p3)
    )

    own = [(f, h) for f in range(nf) for h in range(nh)]
    for a in range(4):
        sides = make_edges([((f, h), x[a][f, h].astype(F32)) for f, h in own])
        for side in range(2):
            e_out0[side, a] = sides[side]
    pl.semaphore_wait(barrier, 2 * rows_near * cols_near - 1)

    def x_rows(a, cb, g, dt, sender=None, receiver=None):
        return rows_of(x[a].at[:, 0], x[a].at[:, nh - 1], cb, g, dt, sender, receiver)

    def land(k):
        return lambda slot, side: eb.at[k, slot, side]

    s_in = x_rows(0, cb_in, 1, 1, first, second)
    s_in += x_rows(0, cb_in, 0, 0)
    s_in += x_rows(1, cb_in, 1, 0, first, first)
    s_in += [transfer(x0, cb_in.at[1, :, 1 : nh + 1], 0, 0, 1, first, second)]
    s_in += edges_of(lambda side: e_out0.at[side], lambda slot, side: eb0.at[slot, side], 0)
    s_in += edges_of(lambda side: e_out0.at[side, 0], land(0), 1, first, second)
    s_cot = edges_of(lambda side: e_out0.at[side, 3], land(5), 1, second, first)
    s_cot += x_rows(3, cb_cot, 1, 1, second, first)
    s_cot += x_rows(3, cb_cot, 0, 0)
    s_cot += [transfer(x3, cb_cot.at[1, :, 1 : nh + 1], 0, 0, 1, second, first)]
    s_cache = x_rows(2, cb_mid, 1, 0, first, first)
    stage0 = s_in + s_cot + s_cache
    start(stage0)

    for fwd, w in ((0, w_in), (1, w_mid)):
        for ab in range(9):
            block = w[ab].astype(F32)
            turned = w[8 - ab].astype(F32).T
            for t in range(3):
                wts[fwd, t * ch : (t + 1) * ch, ab * ch : (ab + 1) * ch] = block[
                    :, t * ch : (t + 1) * ch
                ].astype(BF)
                wts[2 + fwd, t * ch : (t + 1) * ch, ab * ch : (ab + 1) * ch] = turned[
                    (2 - t) * ch : (3 - t) * ch
                ].astype(BF)
    for f, h in own:
        hid[f, h] = act(x0[f, h].astype(F32), g_in).astype(BF)

    arrive(s_in)

    def held(a):
        return merged(lambda slot, side: eb0.at[slot, side, a])

    e0 = jnp.where(edge_ok, act(held(0), g_in), 0.0)
    e1 = jnp.where(edge_ok, jnp.where(first_tile, held(1), act(merged(land(0)), g_in)), 0.0)
    for f in range(nf):
        for hp in range(np_):
            j = f * 8 + hp
            inner = 1 <= hp <= nh
            tile = hid[f, hp - 1].astype(F32) if inner else act(cb_in[0, f, hp].astype(F32), g_in)
            put(1, nf + f, hp, tile, e0, j)
            there = cb_in[1, f, hp].astype(F32)
            here = x1[f, hp - 1].astype(F32) if inner else there
            put(1, f, hp, jnp.where(first_tile, here, act(there, g_in)), e1, j)
    convolve(1, 0)
    tiles = []
    for f, h in own:
        hidden = (acc[f, h] + b_in).astype(BF)
        hid[f, h] = hidden
        a = act(hidden.astype(F32), g_mid).astype(BF)
        cb_mid[0, f, h + 1] = a
        tiles.append(((f, h), a.astype(F32)))
    sides = make_edges(tiles)
    for side in range(2):
        e_out[0, side] = sides[side]

    def later(k, cb, sender, receiver):
        top, bottom = cb.at[0, :, 1], cb.at[0, :, nh]
        items = rows_of(top, bottom, cb, 1, 1, sender, receiver)
        items += rows_of(top, bottom, cb, 0, 0)
        items += [
            transfer(
                cb.at[0, :, 1 : nh + 1], cb.at[1, :, 1 : nh + 1], 0, 0, 1, sender, receiver
            )
        ]
        source = lambda side: e_out.at[k, side]
        items += edges_of(source, land(1 + 2 * k), 0)
        items += edges_of(source, land(2 + 2 * k), 1, sender, receiver)
        return items

    stage1 = later(0, cb_mid, first, second)
    start(stage1)

    arrive(s_cot)
    e0 = jnp.where(edge_ok, held(3), 0.0)
    e1 = jnp.where(edge_ok, jnp.where(first_tile, merged(land(5)), 0.0), 0.0)
    for f in range(nf):
        for hp in range(np_):
            j = f * 8 + hp
            inner = 1 <= hp <= nh
            tile = x3[f, hp - 1] if inner else cb_cot[0, f, hp]
            put(0, f, hp, tile.astype(F32), e0, j)
            tile = jnp.where(first_tile, cb_cot[1, f, hp].astype(F32), 0.0)
            put(0, nf + f, hp, tile, e1, j)
    convolve(0, 3)
    tiles = []
    for f, h in own:
        d = act_back(hid[f, h].astype(F32), g_mid, acc[f, h]).astype(BF)
        cb_back[0, f, h + 1] = d
        tiles.append(((f, h), d.astype(F32)))
    sides = make_edges(tiles)
    for side in range(2):
        e_out[1, side] = sides[side]
    stage2 = later(1, cb_back, second, first)
    start(stage2)

    arrive(s_cache)
    arrive(stage1)
    e0 = jnp.where(edge_ok, merged(land(1)), 0.0)
    e1 = jnp.where(edge_ok, jnp.where(first_tile, held(2), merged(land(2))), 0.0)
    for f in range(nf):
        for hp in range(np_):
            j = f * 8 + hp
            inner = 1 <= hp <= nh
            put(2, nf + f, hp, cb_mid[0, f, hp].astype(F32), e0, j)
            there = cb_mid[1, f, hp].astype(F32)
            if inner:
                there = jnp.where(first_tile, x2[f, hp - 1].astype(F32), there)
            put(2, f, hp, there, e1, j)
    convolve(2, 1)
    for f, h in own:
        wide[f, pl.ds(h, ch, stride=nh), :] = x0[f, h].astype(F32) + acc[f, h] + b_mid
    for f in range(nf):
        dec[f] = wide[f].astype(BF)

    arrive(stage2)
    e0 = jnp.where(edge_ok, merged(land(3)), 0.0)
    e1 = jnp.where(edge_ok, jnp.where(first_tile, merged(land(4)), 0.0), 0.0)
    for f in range(nf):
        for hp in range(np_):
            j = f * 8 + hp
            put(3, f, hp, cb_back[0, f, hp].astype(F32), e0, j)
            tile = jnp.where(first_tile, cb_back[1, f, hp].astype(F32), 0.0)
            put(3, nf + f, hp, tile, e1, j)
    convolve(3, 2)
    for f, h in own:
        grad[f, pl.ds(h, ch, stride=nh), :] = x3[f, h].astype(F32) + act_back(
            x0[f, h].astype(F32), g_in, acc[f, h]
        )
    leave(stage0 + stage1 + stage2)


def per_device(
    frames, cache_in, cache_mid, gain_in, gain_mid, weight_in, bias_in, weight_mid,
    bias_mid, cotangent,
):
    nf, ch, nh, nw = frames.shape
    x = [v.transpose(0, 2, 1, 3) for v in (frames, cache_in, cache_mid, cotangent)]
    rows = [v.reshape(1, ch) for v in (gain_in, gain_mid, bias_in, bias_mid)]
    k = 3 * ch
    vmem = pl.BlockSpec(memory_space=pltpu.VMEM)
    center = pltpu.VMEM((2, nf, nh + 2, ch, nw), BF)
    copies = 96
    dec, grad = pl.pallas_call(
        functools.partial(kernel, lax.axis_size("ha"), lax.axis_size("wa")),
        out_shape=(
            jax.ShapeDtypeStruct((nf, ch * nh, nw), BF),
            jax.ShapeDtypeStruct((nf, ch * nh, nw), F32),
        ),
        in_specs=[vmem] * 10,
        out_specs=(vmem, vmem),
        scratch_shapes=[
            center, center, center, center,
            pltpu.VMEM((3, 2, 4, 16, nw), BF),
            pltpu.VMEM((6, 3, 2, 16, nw), BF),
            pltpu.VMEM((2, 4, 16, nw), BF),
            pltpu.VMEM((2, 2, 16, nw), BF),
            pltpu.VMEM((4, nf + 2, (nh + 2) * k, nw), BF),
            pltpu.VMEM((4, k, 9 * ch), BF),
            pltpu.VMEM((nf, nh, ch, nw), F32),
            pltpu.VMEM((nf, ch * nh, nw), F32),
            pltpu.VMEM((nf, nh, ch, nw), BF),
            pltpu.SemaphoreType.DMA((copies,)),
            pltpu.SemaphoreType.DMA((copies,)),
        ],
        compiler_params=pltpu.CompilerParams(
            collective_id=0, has_side_effects=True, vmem_limit_bytes=60 << 20
        ),
    )(*x, weight_in.reshape(9, ch, k), weight_mid.reshape(9, ch, k), *rows)
    return dec.reshape(nf, ch, nh, nw), grad.reshape(nf, ch, nh, nw)


def solution(mesh):
    moving = P(("grp", "ta"), None, "ha", "wa")
    cache = P("grp", None, "ha", "wa")
    placed = (moving, cache, cache, P(), P(), P(), P(), P(), P(), moving)
    return jax.shard_map(
        per_device, mesh=mesh, in_specs=placed, out_specs=(moving, moving), check_vma=False
    )
```

```python
import functools

import jax
import jax.numpy as jnp
from jax import lax
from jax.experimental import pallas as pl
from jax.experimental.pallas import tpu as pltpu
from jax.sharding import PartitionSpec as P

epsilon = 1e-06
BF, F32 = jnp.bfloat16, jnp.float32


def act(v, g):
    m = jnp.mean(v * v, axis=0, keepdims=True)
    z = v * lax.rsqrt(m + epsilon) * g
    return z * (1.0 / (1.0 + jnp.exp(-z)))


def act_back(v, g, d):
    m = jnp.mean(v * v, axis=0, keepdims=True)
    r = lax.rsqrt(m + epsilon)
    z = v * r * g
    s = 1.0 / (1.0 + jnp.exp(-z))
    q = g * d * s * (1.0 + z * (1.0 - s))
    return r * q - v * (r * r * r) * jnp.mean(q * v, axis=0, keepdims=True)


def kernel(
    n_ha, n_wa, x0, x1, x2, x3, w_in, w_mid, p0, p1, p2, p3, dec, grad,
    cb_in, cb_cot, cb_mid, cb_back, eb0, eb, e_out0, e_out, stack, wts, acc, wide,
    hid, send, recv,
):
    x = (x0, x1, x2, x3)
    nf, nh, ch, nw = x0.shape
    fold = 16
    np_ = nh + 2
    ha, wa, ta = (lax.axis_index(a) for a in ("ha", "wa", "ta"))
    first, second = ta == 0, ta == 1
    lane = lax.broadcasted_iota(jnp.int32, (ch, nw), 1)
    half = nw // 2
    small_lane = lax.broadcasted_iota(jnp.int32, (fold, nw), 1)
    small_row = small_lane % 8
    slot_row = lane % 8

    def have(dh, dw):
        ok = None
        for step, me, count in ((dh, ha, n_ha), (dw, wa, n_wa)):
            if step:
                this = (me > 0) if step < 0 else (me < count - 1)
                ok = this if ok is None else jnp.logical_and(ok, this)
        return ok

    def both(a, b):
        return b if a is None else a if b is None else jnp.logical_and(a, b)

    def when(cond, fn):
        if cond is None:
            fn()
        else:
            pl.when(cond)(fn)

    def target(dh, dw, dt):
        ids = {}
        if dh:
            ids["ha"] = ha + dh
        if dw:
            ids["wa"] = wa + dw
        if dt:
            ids["ta"] = 1 - ta
        return ids

    steps = [(dh, dw) for dh in (-1, 0, 1) for dw in (-1, 0, 1)]
    barrier = pltpu.get_barrier_semaphore()
    for dh, dw in steps:
        for dt in (0, 1):
            if dh or dw or dt:
                when(
                    have(dh, dw),
                    lambda dh=dh, dw=dw, dt=dt: pl.semaphore_signal(
                        barrier, inc=1, device_id=target(dh, dw, dt),
                        device_id_type=pl.DeviceIdType.MESH,
                    ),
                )
    rows_near = 1 + (ha > 0).astype(jnp.int32) + (ha < n_ha - 1).astype(jnp.int32)
    cols_near = 1 + (wa > 0).astype(jnp.int32) + (wa < n_wa - 1).astype(jnp.int32)

    used = [0]

    def transfer(src, dst, dh, dw, dt, sender=None, receiver=None):
        k = used[0]
        used[0] += 1
        copy = pltpu.make_async_remote_copy(
            src_ref=src, dst_ref=dst, send_sem=send.at[k], recv_sem=recv.at[k],
            device_id=target(dh, dw, dt), device_id_type=pl.DeviceIdType.MESH,
        )
        return copy, both(have(dh, dw), sender), both(have(-dh, -dw), receiver)

    def start(items):
        for copy, s, _ in items:
            when(s, copy.start)

    def arrive(items):
        for copy, _, r in items:
            when(r, copy.wait_recv)

    def leave(items):
        for copy, s, _ in items:
            when(s, copy.wait_send)

    def rows_of(top, bottom, cb, g, dt, sender=None, receiver=None):
        return [
            transfer(bottom, cb.at[g, :, 0], 1, 0, dt, sender, receiver),
            transfer(top, cb.at[g, :, nh + 1], -1, 0, dt, sender, receiver),
        ]

    def edges_of(source, landing, dt, sender=None, receiver=None):
        return [
            transfer(
                source((dw + 1) // 2), landing(1 - dh, (dw + 1) // 2), dh, dw, dt,
                sender, receiver,
            )
            for dh, dw in steps if dw
        ]

    def make_edges(tiles):
        e = jnp.zeros((ch, nw), F32)
        for (f, h), tile in tiles:
            j = f * 8 + h + 1
            e = jnp.where(lane == j, tile[:, :1], e)
            e = jnp.where(lane == half + j, tile[:, nw - 1 :], e)
        out = []
        for side in range(2):
            c = jnp.zeros((fold, nw), F32)
            for i in range(ch // fold):
                part = e[i * fold : (i + 1) * fold]
                shift = (i * 16 - half * side) % nw
                part = pltpu.roll(part, shift, 1) if shift else part
                c = jnp.where(small_lane // 16 == i, part, c)
            out.append(c.astype(BF))
        return out

    up, down, left, right = have(-1, 0), have(1, 0), have(0, -1), have(0, 1)

    def flag(cond):
        return jnp.full((ch, nw), cond.astype(jnp.int32), jnp.int32)

    side_ok = jnp.where(lane < half, flag(right), flag(left))
    row_ok = jnp.where(slot_row == 0, flag(up), jnp.where(slot_row == nh + 1, flag(down), 1))
    edge_ok = (side_ok * row_ok) > 0

    def merged(landing):
        sides = []
        for side in range(2):
            v = [landing(s, side)[...].astype(F32) for s in range(3)]
            m = jnp.where(
                small_row == 0,
                pltpu.roll(v[0], nw - nh, 1),
                jnp.where(small_row == nh + 1, pltpu.roll(v[2], nh, 1), v[1]),
            )
            shifts = [(half * side - i * 16) % nw for i in range(ch // fold)]
            sides.append(
                jnp.concatenate([pltpu.roll(m, t, 1) if t else m for t in shifts], axis=0)
            )
        return jnp.where(lane < half, sides[0], sides[1])

    first_tile, up_tile, down_tile = flag(first) > 0, flag(up) > 0, flag(down) > 0

    def put(conv, fp, hp, tile, edge, j):
        base = hp * 3 * ch
        if hp == 0:
            tile = jnp.where(up_tile, tile, 0.0)
        if hp == nh + 1:
            tile = jnp.where(down_tile, tile, 0.0)
        le = jnp.where(lane == 0, edge[:, half + j : half + j + 1], pltpu.roll(tile, 1, 1))
        ri = jnp.where(lane == nw - 1, edge[:, j : j + 1], pltpu.roll(tile, nw - 1, 1))
        stack[conv, fp, base : base + ch] = le.astype(BF)
        stack[conv, fp, base + ch : base + 2 * ch] = tile.astype(BF)
        stack[conv, fp, base + 2 * ch : base + 3 * ch] = ri.astype(BF)

    def convolve(conv, weight):
        for fp in range(nf + 2):
            taps = [t for t in range(3) if 0 <= fp - t < nf]
            lo, hi = taps[0] * ch, (taps[-1] + 1) * ch
            lhs = wts[weight, lo:hi]
            for h in range(0, nh, 2):
                a = stack[conv, fp, h * 3 * ch : (h + 3) * 3 * ch]
                b = stack[conv, fp, (h + 1) * 3 * ch : (h + 4) * 3 * ch]
                out = jnp.dot(
                    lhs, jnp.concatenate([a, b], axis=1), preferred_element_type=F32
                )
                for i, t in enumerate(taps):
                    f = fp - t
                    for k in range(2):
                        part = out[i * ch : (i + 1) * ch, k * nw : (k + 1) * nw]
                        if t == 0:
                            acc[f, h + k] = part
                        else:
                            acc[f, h + k] += part

    eye = lax.broadcasted_iota(jnp.int32, (ch, ch), 0) == lax.broadcasted_iota(
        jnp.int32, (ch, ch), 1
    )
    g_in, g_mid, b_in, b_mid = (
        jnp.sum(jnp.where(eye, p[...], 0.0), axis=1, keepdims=True) for p in (p0, p1, p2, p3)
    )

    own = [(f, h) for f in range(nf) for h in range(nh)]
    for a in range(4):
        sides = make_edges([((f, h), x[a][f, h].astype(F32)) for f, h in own])
        for side in range(2):
            e_out0[side, a] = sides[side]
    pl.semaphore_wait(barrier, 2 * rows_near * cols_near - 1)

    def x_rows(a, cb, g, dt, sender=None, receiver=None):
        return rows_of(x[a].at[:, 0], x[a].at[:, nh - 1], cb, g, dt, sender, receiver)

    def land(k):
        return lambda slot, side: eb.at[k, slot, side]

    s_in = x_rows(0, cb_in, 1, 1, first, second)
    s_in += x_rows(0, cb_in, 0, 0)
    s_in += x_rows(1, cb_in, 1, 0, first, first)
    s_in += [transfer(x0, cb_in.at[1, :, 1 : nh + 1], 0, 0, 1, first, second)]
    s_in += edges_of(lambda side: e_out0.at[side], lambda slot, side: eb0.at[slot, side], 0)
    s_in += edges_of(lambda side: e_out0.at[side, 0], land(0), 1, first, second)
    s_cot = edges_of(lambda side: e_out0.at[side, 3], land(5), 1, second, first)
    s_cot += x_rows(3, cb_cot, 1, 1, second, first)
    s_cot += x_rows(3, cb_cot, 0, 0)
    s_cot += [transfer(x3, cb_cot.at[1, :, 1 : nh + 1], 0, 0, 1, second, first)]
    s_cache = x_rows(2, cb_mid, 1, 0, first, first)
    stage0 = s_in + s_cot + s_cache
    start(stage0)

    for fwd, w in ((0, w_in), (1, w_mid)):
        for ab in range(9):
            block = w[ab].astype(F32)
            turned = w[8 - ab].astype(F32).T
            for t in range(3):
                wts[fwd, t * ch : (t + 1) * ch, ab * ch : (ab + 1) * ch] = block[
                    :, t * ch : (t + 1) * ch
                ].astype(BF)
                wts[2 + fwd, t * ch : (t + 1) * ch, ab * ch : (ab + 1) * ch] = turned[
                    (2 - t) * ch : (3 - t) * ch
                ].astype(BF)
    for f, h in own:
        hid[f, h] = act(x0[f, h].astype(F32), g_in).astype(BF)

    arrive(s_in)

    def held(a):
        return merged(lambda slot, side: eb0.at[slot, side, a])

    e0 = jnp.where(edge_ok, act(held(0), g_in), 0.0)
    e1 = jnp.where(edge_ok, jnp.where(first_tile, held(1), act(merged(land(0)), g_in)), 0.0)
    for f in range(nf):
        for hp in range(np_):
            j = f * 8 + hp
            inner = 1 <= hp <= nh
            tile = hid[f, hp - 1].astype(F32) if inner else act(cb_in[0, f, hp].astype(F32), g_in)
            put(1, nf + f, hp, tile, e0, j)
            there = cb_in[1, f, hp].astype(F32)
            here = x1[f, hp - 1].astype(F32) if inner else there
            put(1, f, hp, jnp.where(first_tile, here, act(there, g_in)), e1, j)
    convolve(1, 0)
    tiles = []
    for f, h in own:
        hidden = (acc[f, h] + b_in).astype(BF)
        hid[f, h] = hidden
        a = act(hidden.astype(F32), g_mid).astype(BF)
        cb_mid[0, f, h + 1] = a
        tiles.append(((f, h), a.astype(F32)))
    sides = make_edges(tiles)
    for side in range(2):
        e_out[0, side] = sides[side]

    def later(k, cb, sender, receiver):
        top, bottom = cb.at[0, :, 1], cb.at[0, :, nh]
        items = rows_of(top, bottom, cb, 1, 1, sender, receiver)
        items += rows_of(top, bottom, cb, 0, 0)
        items += [
            transfer(
                cb.at[0, :, 1 : nh + 1], cb.at[1, :, 1 : nh + 1], 0, 0, 1, sender, receiver
            )
        ]
        source = lambda side: e_out.at[k, side]
        items += edges_of(source, land(1 + 2 * k), 0)
        items += edges_of(source, land(2 + 2 * k), 1, sender, receiver)
        return items

    stage1 = later(0, cb_mid, first, second)
    start(stage1)

    arrive(s_cot)
    e0 = jnp.where(edge_ok, held(3), 0.0)
    e1 = jnp.where(edge_ok, jnp.where(first_tile, merged(land(5)), 0.0), 0.0)
    for f in range(nf):
        for hp in range(np_):
            j = f * 8 + hp
            inner = 1 <= hp <= nh
            tile = x3[f, hp - 1] if inner else cb_cot[0, f, hp]
            put(0, f, hp, tile.astype(F32), e0, j)
            tile = jnp.where(first_tile, cb_cot[1, f, hp].astype(F32), 0.0)
            put(0, nf + f, hp, tile, e1, j)
    convolve(0, 3)
    tiles = []
    for f, h in own:
        d = act_back(hid[f, h].astype(F32), g_mid, acc[f, h]).astype(BF)
        cb_back[0, f, h + 1] = d
        tiles.append(((f, h), d.astype(F32)))
    sides = make_edges(tiles)
    for side in range(2):
        e_out[1, side] = sides[side]
    stage2 = later(1, cb_back, second, first)
    start(stage2)

    arrive(s_cache)
    arrive(stage1)
    e0 = jnp.where(edge_ok, merged(land(1)), 0.0)
    e1 = jnp.where(edge_ok, jnp.where(first_tile, held(2), merged(land(2))), 0.0)
    for f in range(nf):
        for hp in range(np_):
            j = f * 8 + hp
            inner = 1 <= hp <= nh
            put(2, nf + f, hp, cb_mid[0, f, hp].astype(F32), e0, j)
            there = cb_mid[1, f, hp].astype(F32)
            if inner:
                there = jnp.where(first_tile, x2[f, hp - 1].astype(F32), there)
            put(2, f, hp, there, e1, j)
    convolve(2, 1)
    for f, h in own:
        wide[f, pl.ds(h, ch, stride=nh), :] = x0[f, h].astype(F32) + acc[f, h] + b_mid
    for f in range(nf):
        dec[f] = wide[f].astype(BF)

    arrive(stage2)
    e0 = jnp.where(edge_ok, merged(land(3)), 0.0)
    e1 = jnp.where(edge_ok, jnp.where(first_tile, merged(land(4)), 0.0), 0.0)
    for f in range(nf):
        for hp in range(np_):
            j = f * 8 + hp
            put(3, f, hp, cb_back[0, f, hp].astype(F32), e0, j)
            tile = jnp.where(first_tile, cb_back[1, f, hp].astype(F32), 0.0)
            put(3, nf + f, hp, tile, e1, j)
    convolve(3, 2)
    for f, h in own:
        grad[f, pl.ds(h, ch, stride=nh), :] = x3[f, h].astype(F32) + act_back(
            x0[f, h].astype(F32), g_in, acc[f, h]
        )
    leave(stage0 + stage1 + stage2)


def per_device(
    frames, cache_in, cache_mid, gain_in, gain_mid, weight_in, bias_in, weight_mid,
    bias_mid, cotangent,
):
    nf, ch, nh, nw = frames.shape
    x = [v.transpose(0, 2, 1, 3) for v in (frames, cache_in, cache_mid, cotangent)]
    rows = [v.reshape(1, ch) for v in (gain_in, gain_mid, bias_in, bias_mid)]
    k = 3 * ch
    vmem = pl.BlockSpec(memory_space=pltpu.VMEM)
    center = pltpu.VMEM((2, nf, nh + 2, ch, nw), BF)
    copies = 96
    dec, grad = pl.pallas_call(
        functools.partial(kernel, lax.axis_size("ha"), lax.axis_size("wa")),
        out_shape=(
            jax.ShapeDtypeStruct((nf, ch * nh, nw), BF),
            jax.ShapeDtypeStruct((nf, ch * nh, nw), F32),
        ),
        in_specs=[vmem] * 10,
        out_specs=(vmem, vmem),
        scratch_shapes=[
            center, center, center, center,
            pltpu.VMEM((3, 2, 4, 16, nw), BF),
            pltpu.VMEM((6, 3, 2, 16, nw), BF),
            pltpu.VMEM((2, 4, 16, nw), BF),
            pltpu.VMEM((2, 2, 16, nw), BF),
            pltpu.VMEM((4, nf + 2, (nh + 2) * k, nw), BF),
            pltpu.VMEM((4, k, 9 * ch), BF),
            pltpu.VMEM((nf, nh, ch, nw), F32),
            pltpu.VMEM((nf, ch * nh, nw), F32),
            pltpu.VMEM((nf, nh, ch, nw), BF),
            pltpu.SemaphoreType.DMA((copies,)),
            pltpu.SemaphoreType.DMA((copies,)),
        ],
        compiler_params=pltpu.CompilerParams(
            collective_id=0, has_side_effects=True, vmem_limit_bytes=24 << 20
        ),
    )(*x, weight_in.reshape(9, ch, k), weight_mid.reshape(9, ch, k), *rows)
    return dec.reshape(nf, ch, nh, nw), grad.reshape(nf, ch, nh, nw)


def solution(mesh):
    moving = P(("grp", "ta"), None, "ha", "wa")
    cache = P("grp", None, "ha", "wa")
    placed = (moving, cache, cache, P(), P(), P(), P(), P(), P(), moving)
    return jax.shard_map(
        per_device, mesh=mesh, in_specs=placed, out_specs=(moving, moving), check_vma=False
    )
```
